32 devices in a mesh: kown: 8 (over z, y), qown: 4 (over x, core).
Axes of the slice: x: 2, y: 2, z: 4, core: 2. Of those that a mesh axis runs over, the one named last changes fastest.
Arguments:
- g_coarse: bfloat16 [512, 512, 2, 1280], P('kown', 'qown'), may hold values from -384 to 384
- k_points: int32 [3, 512], replicated, may hold values from 0 to 7, as said below
- q_points: int32 [3, 512], replicated, may hold values from 0 to 7, as said below
- re_cells: int32 [3, 512], replicated, may hold values from -4 to 4, as said below
- rp_cells: int32 [3, 512], replicated, may hold values from -4 to 4, as said below
- rp_degen: int32 [512], replicated, may hold values from 1 to 4
- fine_q: int32 [3, 64], replicated, may hold values from 0 to 31
Outputs:
- fine_g: bfloat16 [512, 64, 2, 1280], P('kown', 'qown')
The draws below stay inside these ranges and needn't reach their ends.
Inputs may be any that keep to these rules, and one draw needn't show every extreme that they name: `k_points`: the columns are the 8**3 points of the coarse grid, each once. `q_points`: the columns are the 8**3 points of the coarse grid, each once. `re_cells`: the columns reduced modulo 8 are the 8**3 points of the grid, each once. `rp_cells`: the columns reduced modulo 8 are the 8**3 points of the grid, each once.
All inputs are finite; a program needn't handle non-finite values.
Results may differ from the reference program's by a relative error of at most 0.0095.
Values may be sent and summed in bfloat16 or wider, within the bound.
No kernel may reach another device: no remote copies, remote signals or barrier semaphores. Data moves between devices by JAX's collectives and lax.ppermute only.
A program may use at most 320 MiB of HBM per device.

```python
import jax
import jax.numpy as jnp
import numpy as np
from jax import lax

GRID = 8
FGRID = 32
PAIRS = 1280
NK = 512
NQ = 512
NR = 512
QF = 64


def grid_points(key):
    shuffled = jax.random.permutation(key, GRID ** 3).astype(jnp.int32)
    return jnp.stack([shuffled // (GRID * GRID), shuffled // GRID % GRID, shuffled % GRID], axis=0).astype(jnp.int32)


def lattice(key):
    points = grid_points(jax.random.fold_in(key, 0))
    midpoint = GRID // 2
    centred = points - GRID * (points >= midpoint).astype(jnp.int32)
    flipped = jax.random.randint(jax.random.fold_in(key, 1), points.shape, 0, 2).astype(jnp.int32)
    return (centred + GRID * flipped * (centred == -midpoint).astype(jnp.int32)).astype(jnp.int32)


def draw_k_points(key, part):
    return grid_points(jax.random.fold_in(key, 11))


def draw_q_points(key, part):
    return grid_points(jax.random.fold_in(key, 12))


def draw_re_cells(key, part):
    return lattice(jax.random.fold_in(key, 21))


def draw_rp_cells(key, part):
    return lattice(jax.random.fold_in(key, 22))


def place_ends(values, rng, smallest, high):
    shape = values.shape
    place = [jax.random.randint(jax.random.fold_in(rng, axis), (), 0, shape[axis]) for axis in range(len(shape))]
    values = values.at[tuple(place)].set(smallest)
    longest = shape.index(max(shape))
    place[longest] = (place[longest] + 1) % shape[longest]
    return values.at[tuple(place)].set(high)


def shard_levels(key, dims, pieces, low, top_value):
    loudness = 1.0
    for axis_at, shards_of in pieces:
        steps = jax.random.uniform(jax.random.fold_in(jax.random.fold_in(key, 6), axis_at), (shards_of,), jnp.float32, low / len(pieces), top_value / len(pieces))
        loudness = loudness * jnp.repeat(jnp.exp(steps), dims[axis_at] // shards_of).reshape((-1,) + (1,) * (len(dims) - 1 - axis_at))
    return loudness


def scatter_about(stream_key, shape, deviation, limit, split=(), held_as=jnp.bfloat16):
    array = jax.random.normal(stream_key, shape, jnp.float32) * deviation
    if len(split) > 0:
        array = shard_levels(stream_key, shape, split, -0.22, 0.18) * array
    return jnp.clip(array, min=-limit, max=limit).astype(held_as)


def setup_inputs(seed: int = 0) -> dict:
    arg_keys = jax.random.split(jax.random.key(seed), 8)
    g_coarse = scatter_about(arg_keys[0], (NK, NQ, 2, PAIRS), 64.0, 384.0, ((0, 8), (1, 4)))
    k_points = draw_k_points(jax.random.fold_in(arg_keys[7], 71), 0)
    q_points = draw_q_points(jax.random.fold_in(arg_keys[7], 71), 0)
    re_cells = draw_re_cells(jax.random.fold_in(arg_keys[7], 71), 0)
    rp_cells = draw_rp_cells(jax.random.fold_in(arg_keys[7], 71), 0)
    rp_degen = place_ends(jax.random.randint(arg_keys[5], (NR,), 1, 5), jax.random.fold_in(arg_keys[5], 1), 1, 4).astype(jnp.int32)
    fine_q = place_ends(jax.random.randint(arg_keys[6], (3, QF), 0, FGRID), jax.random.fold_in(arg_keys[6], 1), 0, FGRID - 1).astype(jnp.int32)
    return {"g_coarse": g_coarse, "k_points": k_points, "q_points": q_points, "re_cells": re_cells, "rp_cells": rp_cells, "rp_degen": rp_degen, "fine_q": fine_q}


def circle(modulus):
    angles = 2.0 * np.pi * np.arange(modulus) / modulus
    return (jnp.asarray(np.cos(angles).astype(np.float32)), jnp.asarray(np.sin(angles).astype(np.float32)))


def lookup(turn_index, lookup_table):
    levels = jnp.arange(lookup_table.shape[0], dtype=jnp.int32)
    return jnp.sum(jnp.where(turn_index[..., None] == levels, lookup_table, jnp.zeros_like(lookup_table)), axis=-1)


def phases(left_ints, right_ints, modulus, factor):
    turn_count = jnp.mod(jnp.sum(left_ints[:, :, None] * right_ints[:, None, :], axis=0), modulus).astype(jnp.int32)
    cosine, sine_vals = circle(modulus)
    return ((lookup(turn_count, cosine) * factor).astype(jnp.bfloat16), (lookup(turn_count, sine_vals) * factor).astype(jnp.bfloat16))


def combine(former, latter):
    real_part = former[:, :, 0] + latter[:, :, 1]
    imag_part = former[:, :, 1] - latter[:, :, 0]
    return jnp.stack([real_part, imag_part], axis=2)


def transform_rows(cosine, sine_vals, operand):
    flattened = operand.reshape(operand.shape[0], -1)
    shape_out = (cosine.shape[0],) + operand.shape[1:]
    former = jnp.dot(cosine, flattened, preferred_element_type=jnp.float32).reshape(shape_out)
    latter = jnp.dot(sine_vals, flattened, preferred_element_type=jnp.float32).reshape(shape_out)
    return combine(former, latter).astype(jnp.bfloat16)


def reference(g_coarse, k_points, q_points, re_cells, rp_cells, rp_degen, fine_q):
    k_cosine, k_sine = phases(re_cells, k_points, GRID, 1.0 / NK)
    q_cosine, q_sine = phases(rp_cells, q_points, GRID, 1.0 / NQ)
    weights = 1.0 / rp_degen.astype(jnp.float32)
    f_cosine, f_sine = phases(fine_q, rp_cells, FGRID, weights[None, :])
    f_sine = -f_sine
    q_width = 32

    def k_block(offset):
        window = lax.dynamic_slice_in_dim(g_coarse, offset, q_width, 1)
        return transform_rows(k_cosine, k_sine, window)

    starts = jnp.arange(NQ // q_width, dtype=jnp.int32) * q_width
    stacked = lax.map(k_block, starts)
    g_eq = jnp.moveaxis(stacked, 0, 1).reshape(NR, NQ, 2, PAIRS)
    g_eq = lax.optimization_barrier(g_eq)
    qc_wide = q_cosine.astype(jnp.float32)
    qs_wide = q_sine.astype(jnp.float32)
    fc_wide = f_cosine.astype(jnp.float32)
    fs_wide = f_sine.astype(jnp.float32)
    e_width = 16

    def cell_block(offset):
        window = lax.dynamic_slice_in_dim(g_eq, offset, e_width, 0).astype(jnp.float32)
        former = jnp.einsum("rq,eqcp->ercp", qc_wide, window)
        latter = jnp.einsum("rq,eqcp->ercp", qs_wide, window)
        g_ep = combine(former, latter).astype(jnp.bfloat16)
        g_ep = lax.optimization_barrier(g_ep)
        widened = g_ep.astype(jnp.float32)
        former = jnp.einsum("fr,ercp->efcp", fc_wide, widened)
        latter = jnp.einsum("fr,ercp->efcp", fs_wide, widened)
        return combine(former, latter).astype(jnp.bfloat16)

    offsets = jnp.arange(NR // e_width, dtype=jnp.int32) * e_width
    result = lax.map(cell_block, offsets)
    return result.reshape(NR, QF, 2, PAIRS)
```

```python
import functools

import jax
import jax.numpy as jnp
import numpy as np
from jax import lax
from jax.experimental import pallas as pl
from jax.experimental.pallas import tpu as pltpu
from jax.sharding import PartitionSpec as P

GRID = 8
FGRID = 32
LANES = 128
BF16 = jnp.bfloat16
F32 = jnp.float32


def cosines(turns, modulus):
    table = np.cos(2.0 * np.pi * np.arange(modulus) / modulus).astype(np.float32)
    turns = turns & (modulus - 1)
    turns = jnp.minimum(turns, modulus - turns)
    value = jnp.full(turns.shape, table[0], F32)
    for level in range(1, modulus // 2 + 1):
        value = jnp.where(turns == level, table[level], value)
    return value


def spread(coordinates, count, index_of):
    shape = (coordinates.shape[1], count)
    wanted = index_of(lax.broadcasted_iota(jnp.int32, shape, 1))
    chosen = (lax.broadcasted_iota(jnp.int32, shape, 0) == wanted).astype(F32).astype(BF16)
    return jnp.dot(coordinates.astype(F32).astype(BF16), chosen, preferred_element_type=F32).astype(BF16)


def products(left, right):
    turns = lax.dot_general(left, right, (((0,), (0,)), ((), ())), preferred_element_type=F32)
    return turns.astype(jnp.int32)


def odd(shape, axis):
    return lax.broadcasted_iota(jnp.int32, shape, axis) & 1


def fine_weights(kown, qown, near, fine_q, rp_cells, rp_degen, q_points):
    f_total, cells, q_total = fine_q.shape[1], rp_cells.shape[1], q_points.shape[1]
    q_count = q_total // qown if near else q_total

    def kernel(f_ref, rp_ref, degen_ref, q_ref, out_ref):
        first = lax.axis_index("qown") * q_count if near else 0
        block = f_total // qown

        def fine_index(n):
            if not near:
                return n >> 1
            owner = n // (2 * block)
            owner = ((owner & 1) * (qown // 2) + (owner >> 1)) ^ lax.axis_index("qown")
            return owner * block + ((n >> 1) & (block - 1))

        rp = rp_ref[...].astype(F32).astype(BF16)
        fine = spread(f_ref[...], 2 * f_total, fine_index)
        q_near = spread(q_ref[...], 2 * q_count, lambda n: (n >> 1) + first)
        f_turns = products(fine, rp)
        q_turns = products(rp, q_near)
        scale = 1.0 / degen_ref[...].astype(F32)
        total = jnp.zeros((2 * f_total, 2 * q_count), F32)
        for part in range(2):
            f_part = cosines(f_turns + (FGRID // 4) * (part - odd(f_turns.shape, 0)), FGRID) * scale
            q_part = cosines(q_turns + (GRID // 4) * (part - odd(q_turns.shape, 1)), GRID) * (1.0 / q_total)
            total += jnp.dot(f_part.astype(BF16), q_part.astype(BF16), preferred_element_type=F32)
        out_ref[...] = total.astype(BF16)

    return pl.pallas_call(
        kernel,
        out_shape=jax.ShapeDtypeStruct((2 * f_total, 2 * q_count), BF16),
        compiler_params=pltpu.CompilerParams(vmem_limit_bytes=24 << 20),
        name="fine_weights",
    )(fine_q, rp_cells, rp_degen.reshape(1, cells), q_points)


def k_phases(kown, near, re_cells, k_points):
    cells, points = re_cells.shape[1], k_points.shape[1]
    rows = 2 * cells // kown

    def kernel(re_ref, k_ref, out_ref, columns):
        at = pl.program_id(0)
        me_k = lax.axis_index("kown") if near else 0

        @pl.when(at == 0)
        def _():
            columns[...] = spread(k_ref[...], 2 * points, lambda n: n >> 1)

        row = spread(re_ref[...], rows, lambda n: (n >> 1) + (at ^ me_k) * (cells // kown))
        turns = products(row, columns[...])
        quarter = (GRID // 4) * (odd(turns.shape, 0) - odd(turns.shape, 1))
        out_ref[...] = (cosines(turns + quarter, GRID) * (1.0 / points)).astype(BF16)

    return pl.pallas_call(
        kernel,
        grid=(kown,),
        in_specs=[pl.BlockSpec(re_cells.shape, lambda i: (0, 0)), pl.BlockSpec(k_points.shape, lambda i: (0, 0))],
        out_specs=pl.BlockSpec((rows, 2 * points), lambda i: (i, 0)),
        out_shape=jax.ShapeDtypeStruct((2 * cells, 2 * points), BF16),
        scratch_shapes=[pltpu.VMEM((3, 2 * points), BF16)],
        compiler_params=pltpu.CompilerParams(vmem_limit_bytes=24 << 20),
        name="k_phases",
    )(re_cells, k_points)


def interpolate(weights, g, start, width, pairs, per_pair):
    k_count, q_count = g.shape[:2]
    step = 8
    half = weights.shape[0] // 2

    def kernel(w_ref, g_ref, *out_refs):
        for at in range(step):
            operand = g_ref[at].reshape(2 * q_count, width)
            product = jnp.dot(w_ref[...], operand, preferred_element_type=F32).astype(BF16)
            for core in range(2):
                block = product[core * half : (core + 1) * half]
                out_refs[core][:, :, :, at] = block.reshape(2, pairs, per_pair, 2, width)

    shape = jax.ShapeDtypeStruct((2, pairs, per_pair, k_count, 2, width), BF16)
    return pl.pallas_call(
        kernel,
        grid=(k_count // step,),
        in_specs=[
            pl.BlockSpec(weights.shape, lambda i: (0, 0)),
            pl.BlockSpec(
                (pl.Element(step), pl.Element(q_count), pl.Element(2), pl.Element(width)),
                lambda i: (i * step, 0, 0, start),
            ),
        ],
        out_specs=[pl.BlockSpec((2, pairs, per_pair, step, 2, width), lambda i: (0, 0, 0, i, 0, 0))] * 2,
        out_shape=[shape] * 2,
        compiler_params=pltpu.CompilerParams(vmem_limit_bytes=12 << 20),
        name="interpolate",
    )(weights, g)


def add(name, which, *arrays):
    pairs, per_pair, k_count, _, width = arrays[0].shape[-5:]
    step = 16

    def kernel(*refs):
        for pair in range(pairs):
            for j in range(per_pair):
                total = sum(ref[pair, j].reshape(2 * step, width).astype(F32) for ref in refs[:-1])
                refs[-1][pair, j] = total.astype(BF16).reshape(step, 2, width)

    block = (pairs, per_pair, step, 2, width)
    whole = pl.BlockSpec(block, lambda i: (0, 0, i, 0, 0))
    part = pl.BlockSpec((pl.Squeezed(),) + block, lambda i: (which, 0, 0, i, 0, 0))
    return pl.pallas_call(
        kernel,
        grid=(k_count // step,),
        in_specs=[part if array.ndim == 6 else whole for array in arrays],
        out_specs=whole,
        out_shape=jax.ShapeDtypeStruct(arrays[0].shape[-5:], BF16),
        compiler_params=pltpu.CompilerParams(vmem_limit_bytes=8 << 20),
        name=name,
    )(*arrays)


def to_cells(k_matrix, rows):
    owners, per_pair, k_count, _, width = rows.shape

    def kernel(m_ref, in_ref, *out_refs):
        operand = in_ref[:, 0].reshape(owners * 2 * k_count, width)
        for at in range(owners):
            part = m_ref[at * 2 * k_count : (at + 1) * 2 * k_count, :]
            product = jnp.dot(part, operand, preferred_element_type=F32).astype(BF16)
            out_refs[at][:, 0] = product.reshape(k_count, 2, width)

    return pl.pallas_call(
        kernel,
        grid=(per_pair,),
        in_specs=[
            pl.BlockSpec(k_matrix.shape, lambda j: (0, 0)),
            pl.BlockSpec((owners, 1, k_count, 2, width), lambda j: (0, j, 0, 0, 0)),
        ],
        out_specs=[pl.BlockSpec((k_count, 1, 2, width), lambda j: (0, j, 0, 0))] * owners,
        out_shape=[jax.ShapeDtypeStruct((k_count, per_pair, 2, width), BF16)] * owners,
        compiler_params=pltpu.CompilerParams(vmem_limit_bytes=16 << 20),
        name="to_cells",
    )(k_matrix, rows)


def place(blocks, start, total, out):
    cells, per_pair, _, width = blocks[0].shape
    count = len(blocks)
    step = 16
    given = [] if out is None else [out]

    def kernel(*refs):
        ins, out_ref = refs[:count], refs[-1]
        me = lax.axis_index("kown")
        for at in range(count):
            out_ref[:, pl.ds((me ^ at) * per_pair, per_pair)] = ins[at][...]

    return pl.pallas_call(
        kernel,
        grid=(cells // step,),
        in_specs=[pl.BlockSpec((step, per_pair, 2, width), lambda i: (i, 0, 0, 0))] * count
        + [pl.BlockSpec(memory_space=pl.ANY)] * len(given),
        out_specs=pl.BlockSpec(
            (pl.Element(step), pl.Element(count * per_pair), pl.Element(2), pl.Element(width)),
            lambda i: (i * step, 0, 0, start),
        ),
        out_shape=jax.ShapeDtypeStruct((cells, count * per_pair, 2, total), BF16),
        input_output_aliases={} if out is None else {count: 0},
        compiler_params=pltpu.CompilerParams(vmem_limit_bytes=8 << 20),
        name="place",
    )(*blocks, *given)


def swap(array, axis, size, bit):
    return lax.ppermute(array, axis, [(i, i ^ bit) for i in range(size)])


def chunks_of(pairs):
    tiles = pairs // LANES
    sizes = [1, 3, 3]
    sizes = sizes + [tiles - sum(sizes)] if tiles > sum(sizes) else [tiles]
    starts = np.concatenate([[0], np.cumsum(sizes)[:-1]])
    return [(int(a) * LANES, int(b) * LANES) for a, b in zip(starts, sizes)]


def after(array, *others):
    return lax.optimization_barrier((array, *others))[0]


def order_of(count):
    order = [("S", 0), ("S", 1), ("C", 0), ("M", 0), ("C", 1), ("X", 0), ("S", 2), ("K", 0), ("C", 2), ("X", 1)]
    for at in range(1, count):
        order += [("S", at + 2), ("C", at + 2), ("X", at + 1), ("P", at - 1), ("K", at)]
    return order + [("P", count - 1)]


def pipelined(kown, qown, g, k_points, q_points, re_cells, rp_cells, rp_degen, fine_q):
    per_pair = fine_q.shape[1] // (qown * kown)
    chunks = chunks_of(g.shape[3])
    count = len(chunks)
    kept, near, sent, far, summed, rows, cells, done = {}, {}, {}, {}, {}, {}, {}, {-1: None}
    weights = fine_weights(kown, qown, True, fine_q, rp_cells, rp_degen, q_points)
    last = weights
    k_matrix = None

    def over_q(at):
        nonlocal last
        start, width = chunks[at]
        kept[at], send = interpolate(after(weights, last), g, start, width, kown, per_pair)
        near[at] = swap(send, "qown", qown, 1)
        last = kept[at]

    def add_core(at):
        nonlocal last
        sent[at] = add("add_core", 1, kept[at], after(near[at], last))
        gates = [far[at - 1]] if at == 1 and True else []
        far[at] = swap(after(sent[at], *gates), "qown", qown, 2)
        last = sent[at]

    def add_x(at):
        nonlocal last
        summed[at] = add("add_x", 0, kept[at], near[at], after(far[at], last))
        rows[at] = lax.all_to_all(summed[at], "kown", split_axis=0, concat_axis=0, tiled=True)
        last = summed[at]

    def over_k(at):
        nonlocal last
        cells[at] = to_cells(k_matrix, after(rows[at], last))
        last = cells[at][0]

    def finish(at):
        nonlocal last
        blocks = [block if by == 0 else swap(block, "kown", kown, by) for by, block in enumerate(cells[at])]
        blocks[-1] = after(blocks[-1], last)
        done[at] = place(blocks, chunks[at][0], g.shape[3], done[at - 1])
        if at + 1 < count:
            last, done[at] = lax.optimization_barrier((last, done[at]))

    stages = {"S": over_q, "C": add_core, "X": add_x, "K": over_k, "P": finish}
    for stage, at in order_of(count):
        if stage == "M":
            k_matrix = k_phases(kown, True, after(re_cells, last), k_points)
            last = k_matrix
        elif at < count:
            stages[stage](at)
    return done[count - 1]


def gathered(kown, qown, g, k_points, q_points, re_cells, rp_cells, rp_degen, fine_q):
    q_total, k_total = q_points.shape[1], k_points.shape[1]
    weights = fine_weights(kown, qown, False, fine_q, rp_cells, rp_degen, q_points)
    k_matrix = k_phases(kown, False, re_cells, k_points)
    done = []
    for start in range(0, g.shape[3], 2 * LANES):
        some = after(g, *done)[..., start : start + 2 * LANES]
        rows = lax.all_to_all(some, "qown", split_axis=0, concat_axis=1, tiled=True)
        rows = rows.reshape(rows.shape[0], 2 * q_total, -1)
        fine = jnp.einsum("fq,kqp->kfp", weights, rows, preferred_element_type=F32).astype(BF16)
        fine = lax.all_to_all(fine, "qown", split_axis=1, concat_axis=0, tiled=True)
        fine = lax.all_to_all(fine, "kown", split_axis=1, concat_axis=0, tiled=True)
        fine = fine.reshape(k_total, -1, 2, rows.shape[2]).swapaxes(0, 1).reshape(-1, 2 * k_total, rows.shape[2])
        cells = jnp.einsum("rk,fkp->frp", k_matrix, fine, preferred_element_type=F32).astype(BF16)
        done.append(lax.all_to_all(cells, "kown", split_axis=1, concat_axis=0, tiled=True))
    cells = jnp.concatenate(done, axis=2)
    return cells.reshape(cells.shape[0], -1, 2, g.shape[3]).swapaxes(0, 1)


def solution(mesh):
    kown, qown = mesh.shape["kown"], mesh.shape["qown"]

    def per_device(g_coarse, *rest):
        few = rest[-1].shape[1] <= g_coarse.shape[1]
        form = pipelined if few and qown == 4 else gathered
        return form(kown, qown, g_coarse, *rest)

    return jax.shard_map(
        per_device,
        mesh=mesh,
        in_specs=(P("kown", "qown", None, None), P(), P(), P(), P(), P(), P()),
        out_specs=P("kown", "qown", None, None),
        check_vma=False,
    )
```

```python
import functools

import jax
import jax.numpy as jnp
import numpy as np
from jax import lax
from jax.experimental import pallas as pl
from jax.experimental.pallas import tpu as pltpu
from jax.sharding import PartitionSpec as P

GRID = 8
FGRID = 32
LANES = 128
BF16 = jnp.bfloat16
F32 = jnp.float32


def cosines(turns, modulus):
    table = np.cos(2.0 * np.pi * np.arange(modulus) / modulus).astype(np.float32)
    turns = turns & (modulus - 1)
    turns = jnp.minimum(turns, modulus - turns)
    value = jnp.full(turns.shape, table[0], F32)
    for level in range(1, modulus // 2 + 1):
        value = jnp.where(turns == level, table[level], value)
    return value


def spread(coordinates, count, index_of):
    shape = (coordinates.shape[1], count)
    wanted = index_of(lax.broadcasted_iota(jnp.int32, shape, 1))
    chosen = (lax.broadcasted_iota(jnp.int32, shape, 0) == wanted).astype(F32).astype(BF16)
    return jnp.dot(coordinates.astype(F32).astype(BF16), chosen, preferred_element_type=F32).astype(BF16)


def products(left, right):
    turns = lax.dot_general(left, right, (((0,), (0,)), ((), ())), preferred_element_type=F32)
    return turns.astype(jnp.int32)


def odd(shape, axis):
    return lax.broadcasted_iota(jnp.int32, shape, axis) & 1


def fine_weights(kown, qown, near, fine_q, rp_cells, rp_degen, q_points):
    f_total, cells, q_total = fine_q.shape[1], rp_cells.shape[1], q_points.shape[1]
    q_count = q_total // qown if near else q_total

    def kernel(f_ref, rp_ref, degen_ref, q_ref, out_ref):
        mask, first = 0, 0
        if near:
            me_k, me_q = lax.axis_index("kown"), lax.axis_index("qown")
            mask = (me_q * kown + me_k) * (f_total // (qown * kown))
            first = me_q * q_count
        rp = rp_ref[...].astype(F32).astype(BF16)
        fine = spread(f_ref[...], 2 * f_total, lambda n: (n >> 1) ^ mask)
        q_near = spread(q_ref[...], 2 * q_count, lambda n: (n >> 1) + first)
        f_turns = products(fine, rp)
        q_turns = products(rp, q_near)
        scale = 1.0 / degen_ref[...].astype(F32)
        total = jnp.zeros((2 * f_total, 2 * q_count), F32)
        for part in range(2):
            f_part = cosines(f_turns + (FGRID // 4) * (part - odd(f_turns.shape, 0)), FGRID) * scale
            q_part = cosines(q_turns + (GRID // 4) * (part - odd(q_turns.shape, 1)), GRID) * (1.0 / q_total)
            total += jnp.dot(f_part.astype(BF16), q_part.astype(BF16), preferred_element_type=F32)
        out_ref[...] = total.astype(BF16)

    return pl.pallas_call(
        kernel,
        out_shape=jax.ShapeDtypeStruct((2 * f_total, 2 * q_count), BF16),
        compiler_params=pltpu.CompilerParams(vmem_limit_bytes=24 << 20),
        name="fine_weights",
    )(fine_q, rp_cells, rp_degen.reshape(1, cells), q_points)


def k_phases(kown, near, re_cells, k_points):
    cells, points = re_cells.shape[1], k_points.shape[1]
    rows = 2 * cells // kown

    def kernel(re_ref, k_ref, out_ref, columns):
        at = pl.program_id(0)
        me_k = lax.axis_index("kown") if near else 0

        @pl.when(at == 0)
        def _():
            columns[...] = spread(k_ref[...], 2 * points, lambda n: (n >> 1) ^ (me_k * (points // kown)))

        row = spread(re_ref[...], rows, lambda n: (n >> 1) + (at ^ me_k) * (cells // kown))
        turns = products(row, columns[...])
        quarter = (GRID // 4) * (odd(turns.shape, 0) - odd(turns.shape, 1))
        out_ref[...] = (cosines(turns + quarter, GRID) * (1.0 / points)).astype(BF16)

    return pl.pallas_call(
        kernel,
        grid=(kown,),
        in_specs=[pl.BlockSpec(re_cells.shape, lambda i: (0, 0)), pl.BlockSpec(k_points.shape, lambda i: (0, 0))],
        out_specs=pl.BlockSpec((rows, 2 * points), lambda i: (i, 0)),
        out_shape=jax.ShapeDtypeStruct((2 * cells, 2 * points), BF16),
        scratch_shapes=[pltpu.VMEM((3, 2 * points), BF16)],
        compiler_params=pltpu.CompilerParams(vmem_limit_bytes=24 << 20),
        name="k_phases",
    )(re_cells, k_points)


def interpolate(weights, g, start, width, parts, pairs, per_pair):
    k_count, q_count = g.shape[:2]
    step = 8
    rows = pairs * per_pair * 2

    def kernel(w_ref, g_ref, *out_refs):
        for at in range(step):
            operand = g_ref[at].reshape(2 * q_count, width)
            product = jnp.dot(w_ref[...], operand, preferred_element_type=F32).astype(BF16)
            for part in range(parts):
                block = product[part * rows : (part + 1) * rows]
                out_refs[part][:, :, at] = block.reshape(pairs, per_pair, 2, width)

    shape = jax.ShapeDtypeStruct((pairs, per_pair, k_count, 2, width), BF16)
    return pl.pallas_call(
        kernel,
        grid=(k_count // step,),
        in_specs=[
            pl.BlockSpec(weights.shape, lambda i: (0, 0)),
            pl.BlockSpec(
                (pl.Element(step), pl.Element(q_count), pl.Element(2), pl.Element(width)),
                lambda i: (i * step, 0, 0, start),
            ),
        ],
        out_specs=[pl.BlockSpec((pairs, per_pair, step, 2, width), lambda i: (0, 0, i, 0, 0))] * parts,
        out_shape=[shape] * parts,
        compiler_params=pltpu.CompilerParams(vmem_limit_bytes=12 << 20),
        name="interpolate",
    )(weights, g)


def add_two(former, latter):
    pairs, per_pair, k_count, _, width = former.shape
    step = 16

    def kernel(a_ref, b_ref, out_ref):
        for pair in range(pairs):
            for j in range(per_pair):
                a, b = (ref[pair, j].reshape(2 * step, width).astype(F32) for ref in (a_ref, b_ref))
                out_ref[pair, j] = (a + b).astype(BF16).reshape(step, 2, width)

    spec = pl.BlockSpec((pairs, per_pair, step, 2, width), lambda i: (0, 0, i, 0, 0))
    return pl.pallas_call(
        kernel,
        grid=(k_count // step,),
        in_specs=[spec] * 2,
        out_specs=spec,
        out_shape=jax.ShapeDtypeStruct(former.shape, BF16),
        compiler_params=pltpu.CompilerParams(vmem_limit_bytes=8 << 20),
        name="add_two",
    )(former, latter)


def add_split(one, two, three):
    pairs, per_pair, k_count, _, width = one.shape
    step = 16

    def kernel(a_ref, b_ref, c_ref, *out_refs):
        for pair in range(pairs):
            for j in range(per_pair):
                a, b, c = (ref[pair, j].reshape(2 * step, width).astype(F32) for ref in (a_ref, b_ref, c_ref))
                out_refs[pair][j] = (a + b + c).astype(BF16).reshape(step, 2, width)

    spec = pl.BlockSpec((pairs, per_pair, step, 2, width), lambda i: (0, 0, i, 0, 0))
    return pl.pallas_call(
        kernel,
        grid=(k_count // step,),
        in_specs=[spec] * 3,
        out_specs=[pl.BlockSpec((per_pair, step, 2, width), lambda i: (0, i, 0, 0))] * pairs,
        out_shape=[jax.ShapeDtypeStruct((per_pair, k_count, 2, width), BF16)] * pairs,
        compiler_params=pltpu.CompilerParams(vmem_limit_bytes=8 << 20),
        name="add_split",
    )(one, two, three)


def to_cells(k_matrix, blocks):
    per_pair, k_count, _, width = blocks[0].shape
    count = len(blocks)

    def kernel(m_ref, *refs):
        ins, outs = refs[:count], refs[count:]
        operand = jnp.concatenate([ref[0].reshape(2 * k_count, width) for ref in ins], axis=0)
        for at in range(count):
            rows = m_ref[at * 2 * k_count : (at + 1) * 2 * k_count, :]
            product = jnp.dot(rows, operand, preferred_element_type=F32).astype(BF16)
            outs[at][:, 0] = product.reshape(k_count, 2, width)

    return pl.pallas_call(
        kernel,
        grid=(per_pair,),
        in_specs=[pl.BlockSpec(k_matrix.shape, lambda j: (0, 0))]
        + [pl.BlockSpec((1, k_count, 2, width), lambda j: (j, 0, 0, 0))] * count,
        out_specs=[pl.BlockSpec((k_count, 1, 2, width), lambda j: (0, j, 0, 0))] * count,
        out_shape=[jax.ShapeDtypeStruct((k_count, per_pair, 2, width), BF16)] * count,
        compiler_params=pltpu.CompilerParams(vmem_limit_bytes=16 << 20),
        name="to_cells",
    )(k_matrix, *blocks)


def place(blocks, start, total, out):
    cells, per_pair, _, width = blocks[0].shape
    count = len(blocks)
    step = 16
    given = [] if out is None else [out]

    def kernel(*refs):
        ins, out_ref = refs[:count], refs[-1]
        me = lax.axis_index("kown")
        for at in range(count):
            out_ref[:, pl.ds((me ^ at) * per_pair, per_pair)] = ins[at][...]

    return pl.pallas_call(
        kernel,
        grid=(cells // step,),
        in_specs=[pl.BlockSpec((step, per_pair, 2, width), lambda i: (i, 0, 0, 0))] * count
        + [pl.BlockSpec(memory_space=pl.ANY)] * len(given),
        out_specs=pl.BlockSpec(
            (pl.Element(step), pl.Element(count * per_pair), pl.Element(2), pl.Element(width)),
            lambda i: (i * step, 0, 0, start),
        ),
        out_shape=jax.ShapeDtypeStruct((cells, count * per_pair, 2, total), BF16),
        input_output_aliases={} if out is None else {count: 0},
        compiler_params=pltpu.CompilerParams(vmem_limit_bytes=8 << 20),
        name="place",
    )(*blocks, *given)


def swap(array, axis, size, bit):
    return lax.ppermute(array, axis, [(i, i ^ bit) for i in range(size)])


def chunks_of(pairs):
    tiles = pairs // LANES
    sizes = [3, 4]
    sizes = sizes + [tiles - sum(sizes)] if tiles > sum(sizes) else [tiles]
    starts = np.concatenate([[0], np.cumsum(sizes)[:-1]])
    return [(int(a) * LANES, int(b) * LANES) for a, b in zip(starts, sizes)]


def after(array, *others):
    return lax.optimization_barrier((array, *others))[0]


def pipelined(kown, qown, g, k_points, q_points, re_cells, rp_cells, rp_degen, fine_q):
    per_pair = fine_q.shape[1] // (qown * kown)
    chunks = chunks_of(g.shape[3])
    count = len(chunks)
    weights = fine_weights(kown, qown, True, fine_q, rp_cells, rp_degen, q_points)
    k_matrix = k_phases(kown, True, re_cells, k_points)
    kept, sent, far, summed, cells, done = {}, {}, {}, {}, {}, {-1: None}

    def given(results, at):
        return [results[at]] if at in results else []

    def cross(blocks):
        return [block if by == 0 else swap(block, "kown", kown, by) for by, block in enumerate(blocks)]

    def finish(at):
        done[at] = place(cross(cells[at]), chunks[at][0], g.shape[3], done[at - 1])

    for at, (start, width) in enumerate(chunks):
        gate = after(weights, *given(kept, at - 1), *given(sent, at - 2), *given(summed, at - 2))
        keep, core_keep, x_keep, both = interpolate(gate, g, start, width, qown, kown, per_pair)
        kept[at] = keep
        sent[at] = add_two(x_keep, swap(both, "qown", qown, 1))
        near = swap(core_keep, "qown", qown, 1)
        gates = given(far, at - 1) if 2 == 0 else (given(summed, at - 1) if 2 == 1 or at == 1 else given(summed, at - 2))
        far[at] = swap(after(sent[at], *gates), "qown", qown, 2)
        blocks = add_split(keep, near, far[at])
        summed[at] = blocks[0]
        blocks = [after(block, *[other[0] for other in given(cells, at - 99)]) for block in blocks]
        rows = cross(blocks)
        if at >= 2:
            finish(at - 2)
            rows[0], done[at - 2] = lax.optimization_barrier((rows[0], done[at - 2]))
        cells[at] = to_cells(k_matrix, rows)
    for at in range(count):
        if at not in done:
            finish(at)
    return done[count - 1]


def gathered(kown, qown, g, k_points, q_points, re_cells, rp_cells, rp_degen, fine_q):
    q_total, k_total = q_points.shape[1], k_points.shape[1]
    weights = fine_weights(kown, qown, False, fine_q, rp_cells, rp_degen, q_points)
    k_matrix = k_phases(kown, False, re_cells, k_points)
    done = []
    for start in range(0, g.shape[3], 2 * LANES):
        some = after(g, *done)[..., start : start + 2 * LANES]
        rows = lax.all_to_all(some, "qown", split_axis=0, concat_axis=1, tiled=True)
        rows = rows.reshape(rows.shape[0], 2 * q_total, -1)
        fine = jnp.einsum("fq,kqp->kfp", weights, rows, preferred_element_type=F32).astype(BF16)
        fine = lax.all_to_all(fine, "qown", split_axis=1, concat_axis=0, tiled=True)
        fine = lax.all_to_all(fine, "kown", split_axis=1, concat_axis=0, tiled=True)
        fine = fine.reshape(k_total, -1, 2, rows.shape[2]).swapaxes(0, 1).reshape(-1, 2 * k_total, rows.shape[2])
        cells = jnp.einsum("rk,fkp->frp", k_matrix, fine, preferred_element_type=F32).astype(BF16)
        done.append(lax.all_to_all(cells, "kown", split_axis=1, concat_axis=0, tiled=True))
    cells = jnp.concatenate(done, axis=2)
    return cells.reshape(cells.shape[0], -1, 2, g.shape[3]).swapaxes(0, 1)


def solution(mesh):
    kown, qown = mesh.shape["kown"], mesh.shape["qown"]

    def per_device(g_coarse, *rest):
        few = rest[-1].shape[1] <= g_coarse.shape[1]
        form = pipelined if few and qown == 4 else gathered
        return form(kown, qown, g_coarse, *rest)

    return jax.shard_map(
        per_device,
        mesh=mesh,
        in_specs=(P("kown", "qown", None, None), P(), P(), P(), P(), P(), P()),
        out_specs=P("kown", "qown", None, None),
        check_vma=False,
    )
```

```python
import functools

import jax
import jax.numpy as jnp
import numpy as np
from jax import lax
from jax.experimental import pallas as pl
from jax.experimental.pallas import tpu as pltpu
from jax.sharding import PartitionSpec as P

GRID = 8
FGRID = 32
LANES = 128
BF16 = jnp.bfloat16
F32 = jnp.float32


def cosines(turns, modulus):
    table = np.cos(2.0 * np.pi * np.arange(modulus) / modulus).astype(np.float32)
    turns = turns & (modulus - 1)
    turns = jnp.minimum(turns, modulus - turns)
    value = jnp.full(turns.shape, table[0], F32)
    for level in range(1, modulus // 2 + 1):
        value = jnp.where(turns == level, table[level], value)
    return value


def spread(coordinates, count, index_of):
    shape = (coordinates.shape[1], count)
    wanted = index_of(lax.broadcasted_iota(jnp.int32, shape, 1))
    chosen = (lax.broadcasted_iota(jnp.int32, shape, 0) == wanted).astype(F32).astype(BF16)
    return jnp.dot(coordinates.astype(F32).astype(BF16), chosen, preferred_element_type=F32).astype(BF16)


def products(left, right):
    turns = lax.dot_general(left, right, (((0,), (0,)), ((), ())), preferred_element_type=F32)
    return turns.astype(jnp.int32)


def odd(shape, axis):
    return lax.broadcasted_iota(jnp.int32, shape, axis) & 1


def fine_weights(kown, qown, near, fine_q, rp_cells, rp_degen, q_points):
    f_total, cells, q_total = fine_q.shape[1], rp_cells.shape[1], q_points.shape[1]
    q_count = q_total // qown if near else q_total

    def kernel(f_ref, rp_ref, degen_ref, q_ref, out_ref):
        mask, first = 0, 0
        if near:
            me_k, me_q = lax.axis_index("kown"), lax.axis_index("qown")
            mask = (me_q * kown + me_k) * (f_total // (qown * kown))
            first = me_q * q_count
        rp = rp_ref[...].astype(F32).astype(BF16)
        fine = spread(f_ref[...], 2 * f_total, lambda n: (n >> 1) ^ mask)
        q_near = spread(q_ref[...], 2 * q_count, lambda n: (n >> 1) + first)
        f_turns = products(fine, rp)
        q_turns = products(rp, q_near)
        scale = 1.0 / degen_ref[...].astype(F32)
        total = jnp.zeros((2 * f_total, 2 * q_count), F32)
        for part in range(2):
            f_part = cosines(f_turns + (FGRID // 4) * (part - odd(f_turns.shape, 0)), FGRID) * scale
            q_part = cosines(q_turns + (GRID // 4) * (part - odd(q_turns.shape, 1)), GRID) * (1.0 / q_total)
            total += jnp.dot(f_part.astype(BF16), q_part.astype(BF16), preferred_element_type=F32)
        out_ref[...] = total.astype(BF16)

    return pl.pallas_call(
        kernel,
        out_shape=jax.ShapeDtypeStruct((2 * f_total, 2 * q_count), BF16),
        compiler_params=pltpu.CompilerParams(vmem_limit_bytes=24 << 20),
        name="fine_weights",
    )(fine_q, rp_cells, rp_degen.reshape(1, cells), q_points)


def k_phases(kown, near, re_cells, k_points):
    cells, points = re_cells.shape[1], k_points.shape[1]
    rows = 2 * cells // kown

    def kernel(re_ref, k_ref, out_ref, columns):
        at = pl.program_id(0)
        me_k = lax.axis_index("kown") if near else 0

        @pl.when(at == 0)
        def _():
            columns[...] = spread(k_ref[...], 2 * points, lambda n: (n >> 1) ^ (me_k * (points // kown)))

        row = spread(re_ref[...], rows, lambda n: (n >> 1) + (at ^ me_k) * (cells // kown))
        turns = products(row, columns[...])
        quarter = (GRID // 4) * (odd(turns.shape, 0) - odd(turns.shape, 1))
        out_ref[...] = (cosines(turns + quarter, GRID) * (1.0 / points)).astype(BF16)

    return pl.pallas_call(
        kernel,
        grid=(kown,),
        in_specs=[pl.BlockSpec(re_cells.shape, lambda i: (0, 0)), pl.BlockSpec(k_points.shape, lambda i: (0, 0))],
        out_specs=pl.BlockSpec((rows, 2 * points), lambda i: (i, 0)),
        out_shape=jax.ShapeDtypeStruct((2 * cells, 2 * points), BF16),
        scratch_shapes=[pltpu.VMEM((3, 2 * points), BF16)],
        compiler_params=pltpu.CompilerParams(vmem_limit_bytes=24 << 20),
        name="k_phases",
    )(re_cells, k_points)


def interpolate(weights, g, start, width, parts, pairs, per_pair):
    k_count, q_count = g.shape[:2]
    step = 8
    rows = pairs * per_pair * 2

    def kernel(w_ref, g_ref, *out_refs):
        for at in range(step):
            operand = g_ref[at].reshape(2 * q_count, width)
            product = jnp.dot(w_ref[...], operand, preferred_element_type=F32).astype(BF16)
            for part in range(parts):
                block = product[part * rows : (part + 1) * rows]
                out_refs[part][:, :, at] = block.reshape(pairs, per_pair, 2, width)

    shape = jax.ShapeDtypeStruct((pairs, per_pair, k_count, 2, width), BF16)
    return pl.pallas_call(
        kernel,
        grid=(k_count // step,),
        in_specs=[
            pl.BlockSpec(weights.shape, lambda i: (0, 0)),
            pl.BlockSpec(
                (pl.Element(step), pl.Element(q_count), pl.Element(2), pl.Element(width)),
                lambda i: (i * step, 0, 0, start),
            ),
        ],
        out_specs=[pl.BlockSpec((pairs, per_pair, step, 2, width), lambda i: (0, 0, i, 0, 0))] * parts,
        out_shape=[shape] * parts,
        compiler_params=pltpu.CompilerParams(vmem_limit_bytes=12 << 20),
        name="interpolate",
    )(weights, g)


def add_two(former, latter):
    pairs, per_pair, k_count, _, width = former.shape
    step = 16

    def kernel(a_ref, b_ref, out_ref):
        for pair in range(pairs):
            for j in range(per_pair):
                a, b = (ref[pair, j].reshape(2 * step, width).astype(F32) for ref in (a_ref, b_ref))
                out_ref[pair, j] = (a + b).astype(BF16).reshape(step, 2, width)

    spec = pl.BlockSpec((pairs, per_pair, step, 2, width), lambda i: (0, 0, i, 0, 0))
    return pl.pallas_call(
        kernel,
        grid=(k_count // step,),
        in_specs=[spec] * 2,
        out_specs=spec,
        out_shape=jax.ShapeDtypeStruct(former.shape, BF16),
        compiler_params=pltpu.CompilerParams(vmem_limit_bytes=8 << 20),
        name="add_two",
    )(former, latter)


def add_split(one, two, three):
    pairs, per_pair, k_count, _, width = one.shape
    step = 16

    def kernel(a_ref, b_ref, c_ref, *out_refs):
        for pair in range(pairs):
            for j in range(per_pair):
                a, b, c = (ref[pair, j].reshape(2 * step, width).astype(F32) for ref in (a_ref, b_ref, c_ref))
                out_refs[pair][j] = (a + b + c).astype(BF16).reshape(step, 2, width)

    spec = pl.BlockSpec((pairs, per_pair, step, 2, width), lambda i: (0, 0, i, 0, 0))
    return pl.pallas_call(
        kernel,
        grid=(k_count // step,),
        in_specs=[spec] * 3,
        out_specs=[pl.BlockSpec((per_pair, step, 2, width), lambda i: (0, i, 0, 0))] * pairs,
        out_shape=[jax.ShapeDtypeStruct((per_pair, k_count, 2, width), BF16)] * pairs,
        compiler_params=pltpu.CompilerParams(vmem_limit_bytes=8 << 20),
        name="add_split",
    )(one, two, three)


def to_cells(k_matrix, blocks):
    per_pair, k_count, _, width = blocks[0].shape
    count = len(blocks)

    def kernel(m_ref, *refs):
        ins, outs = refs[:count], refs[count:]
        operand = jnp.concatenate([ref[0].reshape(2 * k_count, width) for ref in ins], axis=0)
        for at in range(count):
            rows = m_ref[at * 2 * k_count : (at + 1) * 2 * k_count, :]
            product = jnp.dot(rows, operand, preferred_element_type=F32).astype(BF16)
            outs[at][:, 0] = product.reshape(k_count, 2, width)

    return pl.pallas_call(
        kernel,
        grid=(per_pair,),
        in_specs=[pl.BlockSpec(k_matrix.shape, lambda j: (0, 0))]
        + [pl.BlockSpec((1, k_count, 2, width), lambda j: (j, 0, 0, 0))] * count,
        out_specs=[pl.BlockSpec((k_count, 1, 2, width), lambda j: (0, j, 0, 0))] * count,
        out_shape=[jax.ShapeDtypeStruct((k_count, per_pair, 2, width), BF16)] * count,
        compiler_params=pltpu.CompilerParams(vmem_limit_bytes=16 << 20),
        name="to_cells",
    )(k_matrix, *blocks)


def place(blocks, start, total, out):
    cells, per_pair, _, width = blocks[0].shape
    count = len(blocks)
    step = 16
    given = [] if out is None else [out]

    def kernel(*refs):
        ins, out_ref = refs[:count], refs[-1]
        me = lax.axis_index("kown")
        for at in range(count):
            out_ref[:, pl.ds((me ^ at) * per_pair, per_pair)] = ins[at][...]

    return pl.pallas_call(
        kernel,
        grid=(cells // step,),
        in_specs=[pl.BlockSpec((step, per_pair, 2, width), lambda i: (i, 0, 0, 0))] * count
        + [pl.BlockSpec(memory_space=pl.ANY)] * len(given),
        out_specs=pl.BlockSpec(
            (pl.Element(step), pl.Element(count * per_pair), pl.Element(2), pl.Element(width)),
            lambda i: (i * step, 0, 0, start),
        ),
        out_shape=jax.ShapeDtypeStruct((cells, count * per_pair, 2, total), BF16),
        input_output_aliases={} if out is None else {count: 0},
        compiler_params=pltpu.CompilerParams(vmem_limit_bytes=8 << 20),
        name="place",
    )(*blocks, *given)


def swap(array, axis, size, bit):
    return lax.ppermute(array, axis, [(i, i ^ bit) for i in range(size)])


def chunks_of(pairs):
    tiles = pairs // LANES
    sizes = [2, 4]
    sizes = sizes + [tiles - sum(sizes)] if tiles > sum(sizes) else [tiles]
    starts = np.concatenate([[0], np.cumsum(sizes)[:-1]])
    return [(int(a) * LANES, int(b) * LANES) for a, b in zip(starts, sizes)]


def after(array, *others):
    return lax.optimization_barrier((array, *others))[0]


def pipelined(kown, qown, g, k_points, q_points, re_cells, rp_cells, rp_degen, fine_q):
    per_pair = fine_q.shape[1] // (qown * kown)
    chunks = chunks_of(g.shape[3])
    count = len(chunks)
    weights = fine_weights(kown, qown, True, fine_q, rp_cells, rp_degen, q_points)
    k_matrix = None
    kept, sent, far, summed, cells, moved, done = {}, {}, {}, {}, {}, {}, {-1: None}

    def given(results, at):
        return [results[at]] if at in results else []

    def cross(blocks):
        moved = {by: swap(blocks[by], "kown", kown, by) for by in sorted(range(1, kown), key=lambda by: (by < kown // 2, by))}
        return [blocks[0]] + [moved[by] for by in range(1, kown)]

    def finish(at):
        done[at] = place(cross(cells[at]), chunks[at][0], g.shape[3], done[at - 1])

    for at, (start, width) in enumerate(chunks):
        gate = after(weights, *given(kept, at - 1), *given(sent, at - 2), *given(summed, at - 2))
        keep, core_keep, x_keep, both = interpolate(gate, g, start, width, qown, kown, per_pair)
        kept[at] = keep
        sent[at] = add_two(x_keep, swap(both, "qown", qown, 1))
        if at == 0:
            k_matrix = k_phases(kown, True, after(re_cells, sent[0]), k_points)
        near = swap(core_keep, "qown", qown, 1)
        gates = given(far, at - 1) if 2 == 0 or (2 == 4 and at > 1) else (given(summed, at - 1) if 2 == 1 or at == 1 else given(summed, at - 2))
        far[at] = swap(after(sent[at], *gates), "qown", qown, 2)
        blocks = add_split(keep, near, far[at])
        summed[at] = blocks[0]
        blocks = [after(block, *[other[0] for other in given(cells, at - 99)]) for block in blocks]
        rows = cross(blocks)
        moved[at] = list(rows)
        if at >= 2:
            finish(at - 2)
            rows[0], done[at - 2] = lax.optimization_barrier((rows[0], done[at - 2]))
        cells[at] = to_cells(k_matrix, rows)
    for at in range(count):
        if at not in done:
            finish(at)
    return done[count - 1]


def gathered(kown, qown, g, k_points, q_points, re_cells, rp_cells, rp_degen, fine_q):
    q_total, k_total = q_points.shape[1], k_points.shape[1]
    weights = fine_weights(kown, qown, False, fine_q, rp_cells, rp_degen, q_points)
    k_matrix = k_phases(kown, False, re_cells, k_points)
    done = []
    for start in range(0, g.shape[3], 2 * LANES):
        some = after(g, *done)[..., start : start + 2 * LANES]
        rows = lax.all_to_all(some, "qown", split_axis=0, concat_axis=1, tiled=True)
        rows = rows.reshape(rows.shape[0], 2 * q_total, -1)
        fine = jnp.einsum("fq,kqp->kfp", weights, rows, preferred_element_type=F32).astype(BF16)
        fine = lax.all_to_all(fine, "qown", split_axis=1, concat_axis=0, tiled=True)
        fine = lax.all_to_all(fine, "kown", split_axis=1, concat_axis=0, tiled=True)
        fine = fine.reshape(k_total, -1, 2, rows.shape[2]).swapaxes(0, 1).reshape(-1, 2 * k_total, rows.shape[2])
        cells = jnp.einsum("rk,fkp->frp", k_matrix, fine, preferred_element_type=F32).astype(BF16)
        done.append(lax.all_to_all(cells, "kown", split_axis=1, concat_axis=0, tiled=True))
    cells = jnp.concatenate(done, axis=2)
    return cells.reshape(cells.shape[0], -1, 2, g.shape[3]).swapaxes(0, 1)


def solution(mesh):
    kown, qown = mesh.shape["kown"], mesh.shape["qown"]

    def per_device(g_coarse, *rest):
        few = rest[-1].shape[1] <= g_coarse.shape[1]
        form = pipelined if few and qown == 4 else gathered
        return form(kown, qown, g_coarse, *rest)

    return jax.shard_map(
        per_device,
        mesh=mesh,
        in_specs=(P("kown", "qown", None, None), P(), P(), P(), P(), P(), P()),
        out_specs=P("kown", "qown", None, None),
        check_vma=False,
    )
```
